32 devices in a mesh: parts: 2 (over y), off: 4 (over z), depth: 2 (over x), shot: 2 (over core).
Axes of the slice: x: 2, y: 2, z: 4, core: 2. Of those that a mesh axis runs over, the one named last changes fastest.
Arguments:
- image: bfloat16 [64, 32, 32, 256], P('off', None, 'depth'), may hold values from -4 to 4
- offset_of: int32 [64], P('off'), may hold values from 0 to 63, each once
- background: bfloat16 [4, 32, 32, 256], P(('parts', 'shot'), 'off', 'depth'), parts along dimension 0, may hold values from -6 to 6
- wave_now: float32 [4, 32, 32, 256], P(('parts', 'shot'), 'off', 'depth'), parts along dimension 0, may hold values from -6 to 6
- wave_prev: float32 [4, 32, 32, 256], P(('parts', 'shot'), 'off', 'depth'), parts along dimension 0, may hold values from -6 to 6
- courant: float32 [32, 32, 256], P('off', 'depth'), may hold values from 0.02 to 0.15
Outputs:
- wave_next: float32 [4, 32, 32, 256], P(('parts', 'shot'), 'off', 'depth'), parts along dimension 0
The draws below stay inside these ranges and needn't reach their ends.
There are 2 independent parts, one for each index of `parts`. The reference program is written for one: setup_inputs(seed, part) draws one part's arguments, and reference() takes and returns one part's arrays. A program takes and returns all parts, laid end to end along the dimension named above; an argument that names none is the same for every part. Nothing has to cross between parts.
Inputs may be any that keep to these rules, and one draw needn't show every extreme that they name: Each value appears once; image column k holds offset offset_of[k] - 32 cells along x.
All inputs are finite; a program needn't handle non-finite values.
Results may differ from the reference program's by a relative error of at most 0.0003.
Values may be sent and summed in bfloat16 or wider, within the bound.
A program may use at most 64 MiB of HBM per device.

```python
import math
import jax
import jax.numpy as jnp
from jax import lax

H = 64
NX = 256
NY = 32
NZ = 32
SHOTS = 2


def spiked(result, own_key, source, target, parts, factor):
    owner, partner = [(jnp.arange(result.shape[dim]) // (result.shape[dim] // parts)).reshape([-1 if axis == dim else 1 for axis in range(result.ndim)]) for dim in (source, target)]
    chosen = jax.random.permutation(own_key, parts)[partner]
    strong = (owner == chosen) | (owner == (partner + parts // 2) % parts)
    return jnp.where(strong, factor * result, result)


def block_levels(stream_key, shape, pieces, least, largest):
    def one(dim, parts):
        steps = jax.random.uniform(jax.random.fold_in(jax.random.fold_in(stream_key, 6), dim), (parts,), jnp.float32, least / len(pieces), largest / len(pieces))
        return jnp.repeat(jnp.exp(steps), shape[dim] // parts).reshape((-1,) + (1,) * (len(shape) - dim - 1))

    factor_of = one(*pieces[0])
    for cut in pieces[1:]:
        factor_of = factor_of * one(*cut)
    return factor_of


def normal_values(stream_key, extent, deviation, limit, cuts=(), dtype=jnp.bfloat16):
    level = block_levels(stream_key, extent, cuts, -0.22, 0.18) if cuts else 1.0
    entries = jax.random.normal(stream_key, extent, jnp.float32) * deviation * level
    return jnp.minimum(jnp.maximum(entries, -limit), limit).astype(dtype)


def heavy_noise(stream_key, shape, spread, reach, cuts, heavy, kind=jnp.bfloat16):
    values = spread * jax.random.normal(stream_key, shape, jnp.float32)
    if cuts:
        values = values * block_levels(stream_key, shape, cuts, -0.22, 0.18)
    return jnp.clip(spiked(values, jax.random.fold_in(stream_key, 3), *heavy), -reach, reach).astype(kind)


def setup_inputs(seed: int = 0, part: int = 0) -> dict:
    keys = jax.random.split(jax.random.key(seed), 7)
    part_keys = jax.random.split(jax.random.fold_in(keys[6], part), 7)
    return {
        "image": heavy_noise(keys[0], (H, NY, NZ, NX), 0.5, 4.0, ((0, 4), (2, 2)), (0, 1, 4, 2.0)),
        "offset_of": jax.random.permutation(keys[1], H).astype(jnp.int32),
        "background": normal_values(part_keys[2], (SHOTS, NY, NZ, NX), 1.0, 6.0, ((0, 2), (1, 4), (2, 2))),
        "wave_now": normal_values(part_keys[3], (SHOTS, NY, NZ, NX), 1.0, 6.0, ((0, 2), (1, 4), (2, 2)), jnp.float32),
        "wave_prev": normal_values(part_keys[4], (SHOTS, NY, NZ, NX), 1.0, 6.0, ((0, 2), (1, 4), (2, 2)), jnp.float32),
        "courant": jnp.clip(jnp.exp(math.log(0.15) - 2.014903 * jax.random.uniform(keys[5], (NY, NZ, NX), jnp.float32) ** block_levels(keys[5], (NY, NZ, NX), ((0, 4), (1, 2)), -0.2, 0.2)), 0.02, 0.15),
    }


STENCIL = (-205.0 / 72.0, 8.0 / 5.0, -1.0 / 5.0, 8.0 / 315.0, -1.0 / 560.0)


def laplace(padded, rows_y, rows_z, cols_x):
    extended = jnp.pad(padded, ((0, 0), (0, 0), (4, 4)))
    centre = extended[4:4 + rows_y, 4:4 + rows_z, 4:4 + cols_x]
    running = 3.0 * STENCIL[0] * centre
    for radius in range(1, 5):
        beside_all = extended[4 + radius:4 + radius + rows_y, 4:4 + rows_z, 4:4 + cols_x]
        beside_all = beside_all + extended[4 - radius:4 - radius + rows_y, 4:4 + rows_z, 4:4 + cols_x]
        beside_all = beside_all + extended[4:4 + rows_y, 4 + radius:4 + radius + rows_z, 4:4 + cols_x]
        beside_all = beside_all + extended[4:4 + rows_y, 4 - radius:4 - radius + rows_z, 4:4 + cols_x]
        beside_all = beside_all + extended[4:4 + rows_y, 4:4 + rows_z, 4 + radius:4 + radius + cols_x]
        beside_all = beside_all + extended[4:4 + rows_y, 4:4 + rows_z, 4 - radius:4 - radius + cols_x]
        running = running + STENCIL[radius] * beside_all
    return running


def reference(image, offset_of, background, wave_now, wave_prev, courant):
    half_span = H // 2

    def one_shot(inputs):
        backdrop, current, previous = inputs
        extended_bg = jnp.pad(backdrop, ((0, 0), (0, 0), (half_span, half_span)))

        def add_column(column, running):
            offset_cells = (offset_of[column] - half_span).astype(jnp.int32)
            image_col = lax.dynamic_index_in_dim(image, column, 0, keepdims=False)
            starts = (jnp.zeros((), jnp.int32), jnp.zeros((), jnp.int32), (half_span - offset_cells).astype(jnp.int32))
            shifted = lax.dynamic_slice(extended_bg, starts, (NY, NZ, NX))
            return running + image_col.astype(jnp.float32) * shifted.astype(jnp.float32)

        source = lax.fori_loop(0, H, add_column, jnp.zeros((NY, NZ, NX), jnp.float32))
        padded = jnp.pad(current, ((4, 4), (4, 4), (0, 0)))
        bending = laplace(padded, NY, NZ, NX)
        return 2.0 * current - previous + courant * (bending + source)

    return lax.map(one_shot, (background, wave_now, wave_prev))
```

```python
import functools

import jax
import jax.numpy as jnp
from jax import lax
from jax.experimental import pallas as pl
from jax.experimental.pallas import tpu as pltpu
from jax.sharding import PartitionSpec as P

H = 64
STENCIL = (-205.0 / 72.0, 8.0 / 5.0, -1.0 / 5.0, 8.0 / 315.0, -1.0 / 560.0)
R = 4
MESH = pl.DeviceIdType.MESH


def kernel(
    n, nd,
    off_ref, img_hbm, bg_hbm, now_hbm, prev_hbm, cour_hbm,
    out_ref,
    img, bg, wext, prev, cour, shift, acc, fin, part_out, part_in,
    load_sem, img_sem, bg_send, bg_recv, halo_send, halo_recv, p_send, p_recv,
):
    K, _, Z, X = img.shape
    Y = out_ref.shape[1]
    me = lax.axis_index("off")
    dep = lax.axis_index("depth")
    has = {"l": me > 0, "r": me < n - 1, "u": dep > 0, "d": dep < nd - 1}
    near = {"l": {"off": me - 1}, "r": {"off": me + 1},
            "u": {"depth": dep - 1}, "d": {"depth": dep + 1}}

    own = wext.at[pl.ds(R, Y), pl.ds(8, Z), :]
    ld_bg = pltpu.make_async_copy(bg_hbm.at[0], bg.at[me], load_sem.at[0])
    ld_now = pltpu.make_async_copy(now_hbm.at[0], own, load_sem.at[1])
    ld_prev = pltpu.make_async_copy(prev_hbm.at[0], prev, load_sem.at[2])
    ld_cour = pltpu.make_async_copy(cour_hbm, cour, load_sem.at[3])
    ld_bg.start()
    ld_now.start()

    def img_load(j):
        rows = pl.ds(j * Y, Y)
        return pltpu.make_async_copy(img_hbm.at[:, rows], img.at[:, rows], img_sem.at[j])

    img_load(me).start()
    for t in range(1, n):
        @pl.when(me - t >= 0)
        def _():
            img_load(me - t).start()

        @pl.when(me + t < n)
        def _():
            img_load(me + t).start()
    ld_prev.start()
    ld_cour.start()

    barrier = pltpu.get_barrier_semaphore()
    for side in "lrud":
        @pl.when(has[side])
        def _():
            pl.semaphore_signal(barrier, inc=1, device_id=near[side], device_id_type=MESH)

    def clear(rows, cols):
        wext[rows, cols, :] = jnp.zeros((rows.size, cols.size, X), jnp.float32)

    edge = {"l": (pl.ds(0, R), pl.ds(8, Z)), "r": (pl.ds(R + Y, R), pl.ds(8, Z)),
            "u": (pl.ds(R, Y), pl.ds(0, 8)), "d": (pl.ds(R, Y), pl.ds(8 + Z, 8))}
    for side in "lrud":
        @pl.when(jnp.logical_not(has[side]))
        def _():
            clear(*edge[side])

    lead = lax.broadcasted_iota(jnp.int32, (X, X), 1) - lax.broadcasted_iota(jnp.int32, (X, X), 0)

    def build(k, carry):
        h = off_ref[k] - H // 2
        shift[k] = jnp.where(lead == h, 1.0, 0.0).astype(jnp.bfloat16)
        return carry

    half = K // 2
    lax.fori_loop(0, half, build, 0)
    ld_bg.wait()
    ld_now.wait()
    count = sum(has[s].astype(jnp.int32) for s in "lrud")
    pl.semaphore_wait(barrier, count)

    def bg_copy(j, side, slot):
        return pltpu.make_async_remote_copy(
            src_ref=bg.at[j], dst_ref=bg.at[j], send_sem=bg_send.at[slot, j],
            recv_sem=bg_recv.at[j], device_id=near[side], device_id_type=MESH)

    mine = {"l": (pl.ds(R, R), pl.ds(8, Z)), "r": (pl.ds(Y, R), pl.ds(8, Z)),
            "u": (pl.ds(R, Y), pl.ds(8, 8)), "d": (pl.ds(R, Y), pl.ds(Z, 8))}
    other = {"l": "r", "r": "l", "u": "d", "d": "u"}
    num = {"l": 0, "r": 1, "u": 2, "d": 3}

    def halo_copy(side):
        there = other[side]
        return pltpu.make_async_remote_copy(
            src_ref=wext.at[mine[side][0], mine[side][1], :],
            dst_ref=wext.at[edge[there][0], edge[there][1], :],
            send_sem=halo_send.at[num[side]], recv_sem=halo_recv.at[num[there]],
            device_id=near[side], device_id_type=MESH)

    for slot, side in enumerate("lr"):
        @pl.when(has[side])
        def _():
            bg_copy(me, side, slot).start()
    for side in "udlr":
        @pl.when(has[side])
        def _():
            halo_copy(side).start()

    lax.fori_loop(half, K, build, 0)

    group = 4 if K % 4 == 0 else 1

    def partial(j, dst, slot):
        lhs = bg[j].reshape(Y * Z, X)
        rows = pl.ds(j * Y, Y)

        def body(g, carry):
            total = None
            for m in range(group):
                k = g * group + m
                moved = jnp.dot(lhs, shift[k], preferred_element_type=jnp.float32)
                term = img[k, rows].astype(jnp.float32) * moved.reshape(Y, Z, X)
                total = term if total is None else total + term

            @pl.when(g == 0)
            def _():
                dst[slot] = total

            @pl.when(g > 0)
            def _():
                dst[slot] = dst[slot] + total
            return carry

        lax.fori_loop(0, K // group, body, 0)

    def part_copy(j):
        return pltpu.make_async_remote_copy(
            src_ref=part_out.at[j], dst_ref=part_in.at[me], send_sem=p_send.at[j],
            recv_sem=p_recv.at[me], device_id={"off": j}, device_id_type=MESH)

    def part_arrival(j):
        return pltpu.make_async_remote_copy(
            src_ref=part_out.at[j], dst_ref=part_in.at[j], send_sem=p_send.at[j],
            recv_sem=p_recv.at[j], device_id={"off": j}, device_id_type=MESH)

    img_load(me).wait()
    partial(me, acc, 0)

    for t in range(1, n):
        for j, ok, onward, slot, side in (
            (me - t, me - t >= 0, me < n - 1, 1, "r"),
            (me + t, me + t < n, me > 0, 0, "l"),
        ):
            @pl.when(ok)
            def _():
                bg_copy(j, side, slot).wait_recv()

                @pl.when(onward)
                def _():
                    bg_copy(j, side, slot).start()
        for j, ok in ((me - t, me - t >= 0), (me + t, me + t < n)):
            @pl.when(ok)
            def _():
                img_load(j).wait()
                partial(j, part_out, j)
                part_copy(j).start()

    ld_prev.wait()
    ld_cour.wait()
    for side in "lrud":
        @pl.when(has[side])
        def _():
            halo_copy(side).wait_send()
            pltpu.make_async_remote_copy(
                src_ref=wext.at[mine[side][0], mine[side][1], :],
                dst_ref=wext.at[edge[side][0], edge[side][1], :],
                send_sem=halo_send.at[num[side]], recv_sem=halo_recv.at[num[side]],
                device_id=near[side], device_id_type=MESH).wait_recv()

    lane = lax.broadcasted_iota(jnp.int32, (Z, X), 1)

    def plane(y, carry):
        centre = wext[y + R, pl.ds(8, Z), :]
        running = 3.0 * STENCIL[0] * centre
        for r in range(1, R + 1):
            beside = wext[y + R + r, pl.ds(8, Z), :] + wext[y + R - r, pl.ds(8, Z), :]
            beside = beside + wext[y + R, pl.ds(8 + r, Z), :]
            beside = beside + wext[y + R, pl.ds(8 - r, Z), :]
            beside = beside + jnp.where(lane < X - r, pltpu.roll(centre, X - r, 1), 0.0)
            beside = beside + jnp.where(lane >= r, pltpu.roll(centre, r, 1), 0.0)
            running = running + STENCIL[r] * beside
        fin[y] = 2.0 * centre - prev[y] + cour[y] * (running + acc[0, y])
        return carry

    lax.fori_loop(0, Y, plane, 0)

    for t in range(1, n):
        for j, ok in ((me - t, me - t >= 0), (me + t, me + t < n)):
            @pl.when(ok)
            def _():
                part_arrival(j).wait_recv()
                fin[...] = fin[...] + cour[...] * part_in[j]
    out_ref[0] = fin[...]

    for slot, side in enumerate("lr"):
        @pl.when(has[side])
        def _():
            bg_copy(me, side, slot).wait_send()
    for t in range(1, n):
        for j, ok, onward, slot, side in (
            (me - t, me - t >= 0, me < n - 1, 1, "r"),
            (me + t, me + t < n, me > 0, 0, "l"),
        ):
            @pl.when(ok)
            def _():
                part_copy(j).wait_send()

                @pl.when(onward)
                def _():
                    bg_copy(j, side, slot).wait_send()


def on_device(n, nd, image, offset_of, background, wave_now, wave_prev, courant):
    K, rows, Z, X = image.shape
    Y = wave_now.shape[1]
    f32 = jnp.float32
    anywhere = pl.BlockSpec(memory_space=pl.ANY)
    dma = pltpu.SemaphoreType.DMA
    return pl.pallas_call(
        functools.partial(kernel, n, nd),
        out_shape=jax.ShapeDtypeStruct(wave_now.shape, f32),
        in_specs=[pl.BlockSpec(memory_space=pltpu.SMEM)] + [anywhere] * 5,
        out_specs=pl.BlockSpec(memory_space=pltpu.VMEM),
        scratch_shapes=[
            pltpu.VMEM((K, rows, Z, X), jnp.bfloat16),
            pltpu.VMEM((n, Y, Z, X), jnp.bfloat16),
            pltpu.VMEM((Y + 2 * R, Z + 16, X), f32),
            pltpu.VMEM((Y, Z, X), f32),
            pltpu.VMEM((Y, Z, X), f32),
            pltpu.VMEM((K, X, X), jnp.bfloat16),
            pltpu.VMEM((1, Y, Z, X), f32),
            pltpu.VMEM((Y, Z, X), f32),
            pltpu.VMEM((n, Y, Z, X), f32),
            pltpu.VMEM((n, Y, Z, X), f32),
            dma((4,)), dma((n,)), dma((2, n)), dma((n,)), dma((4,)), dma((4,)),
            dma((n,)), dma((n,)),
        ],
        compiler_params=pltpu.CompilerParams(
            collective_id=0, has_side_effects=True, vmem_limit_bytes=48 * 2**20),
        name="born_step",
    )(offset_of, image, background, wave_now, wave_prev, courant)


def solution(mesh):
    wave = P(("parts", "shot"), "off", "depth", None)
    return jax.shard_map(
        functools.partial(on_device, mesh.shape["off"], mesh.shape["depth"]),
        mesh=mesh,
        in_specs=(
            P("off", None, "depth", None),
            P("off"),
            wave,
            wave,
            wave,
            P("off", "depth", None),
        ),
        out_specs=wave,
        check_vma=False,
    )
```

```python
import functools

import jax
import jax.numpy as jnp
from jax import lax
from jax.experimental import pallas as pl
from jax.experimental.pallas import tpu as pltpu
from jax.sharding import PartitionSpec as P

H = 64
STENCIL = (-205.0 / 72.0, 8.0 / 5.0, -1.0 / 5.0, 8.0 / 315.0, -1.0 / 560.0)
R = 4
LANES = 128
TOP = 32767.0
MESH = pl.DeviceIdType.MESH


def kernel(
    n, nd,
    off_ref, img_hbm, bg_hbm, now_hbm, prev_hbm, cour_hbm,
    out_ref,
    img, bg, wext, prev, cour, shift, acc, fin, part_out, part_in, scale_out, scale_in,
    load_sem, img_sem, bg_send, bg_recv, halo_send, halo_recv, p_send, p_recv, s_send, s_recv,
):
    K, _, Z, X = img.shape
    Y = out_ref.shape[1]
    me = lax.axis_index("off")
    dep = lax.axis_index("depth")
    has = {"l": me > 0, "r": me < n - 1, "u": dep > 0, "d": dep < nd - 1}
    near = {"l": {"off": me - 1}, "r": {"off": me + 1},
            "u": {"depth": dep - 1}, "d": {"depth": dep + 1}}

    own = wext.at[pl.ds(R, Y), pl.ds(8, Z), :]
    ld_bg = pltpu.make_async_copy(bg_hbm.at[0], bg.at[me], load_sem.at[0])
    ld_now = pltpu.make_async_copy(now_hbm.at[0], own, load_sem.at[1])
    ld_prev = pltpu.make_async_copy(prev_hbm.at[0], prev, load_sem.at[2])
    ld_cour = pltpu.make_async_copy(cour_hbm, cour, load_sem.at[3])
    ld_bg.start()
    ld_now.start()

    def img_load(j):
        rows = pl.ds(j * Y, Y)
        return pltpu.make_async_copy(img_hbm.at[:, rows], img.at[:, rows], img_sem.at[j])

    img_load(me).start()
    for t in range(1, n):
        @pl.when(me - t >= 0)
        def _():
            img_load(me - t).start()

        @pl.when(me + t < n)
        def _():
            img_load(me + t).start()
    ld_prev.start()
    ld_cour.start()

    barrier = pltpu.get_barrier_semaphore()
    for side in "lrud":
        @pl.when(has[side])
        def _():
            pl.semaphore_signal(barrier, inc=1, device_id=near[side], device_id_type=MESH)

    def clear(rows, cols):
        wext[rows, cols, :] = jnp.zeros((rows.size, cols.size, X), jnp.float32)

    edge = {"l": (pl.ds(0, R), pl.ds(8, Z)), "r": (pl.ds(R + Y, R), pl.ds(8, Z)),
            "u": (pl.ds(R, Y), pl.ds(0, 8)), "d": (pl.ds(R, Y), pl.ds(8 + Z, 8))}
    for side in "lrud":
        @pl.when(jnp.logical_not(has[side]))
        def _():
            clear(*edge[side])

    lead = lax.broadcasted_iota(jnp.int32, (X, X), 1) - lax.broadcasted_iota(jnp.int32, (X, X), 0)

    def build(k, carry):
        h = off_ref[k] - H // 2
        shift[k] = jnp.where(lead == h, 1.0, 0.0).astype(jnp.bfloat16)
        return carry

    half = K // 2
    lax.fori_loop(0, half, build, 0)
    ld_bg.wait()
    ld_now.wait()
    count = sum(has[s].astype(jnp.int32) for s in "lrud")
    pl.semaphore_wait(barrier, count)

    def bg_copy(j, side, slot):
        return pltpu.make_async_remote_copy(
            src_ref=bg.at[j], dst_ref=bg.at[j], send_sem=bg_send.at[slot, j],
            recv_sem=bg_recv.at[j], device_id=near[side], device_id_type=MESH)

    mine = {"l": (pl.ds(R, R), pl.ds(8, Z)), "r": (pl.ds(Y, R), pl.ds(8, Z)),
            "u": (pl.ds(R, Y), pl.ds(8, 8)), "d": (pl.ds(R, Y), pl.ds(Z, 8))}
    other = {"l": "r", "r": "l", "u": "d", "d": "u"}
    num = {"l": 0, "r": 1, "u": 2, "d": 3}

    def halo_copy(side):
        there = other[side]
        return pltpu.make_async_remote_copy(
            src_ref=wext.at[mine[side][0], mine[side][1], :],
            dst_ref=wext.at[edge[there][0], edge[there][1], :],
            send_sem=halo_send.at[num[side]], recv_sem=halo_recv.at[num[there]],
            device_id=near[side], device_id_type=MESH)

    for slot, side in enumerate("lr"):
        @pl.when(has[side])
        def _():
            bg_copy(me, side, slot).start()
    for side in "udlr":
        @pl.when(has[side])
        def _():
            halo_copy(side).start()

    lax.fori_loop(half, K, build, 0)

    group = 4 if K % 4 == 0 else 1

    def partial(j, dst, slot):
        lhs = bg[j].reshape(Y * Z, X)
        rows = pl.ds(j * Y, Y)

        def body(g, carry):
            total = None
            for m in range(group):
                k = g * group + m
                moved = jnp.dot(lhs, shift[k], preferred_element_type=jnp.float32)
                term = img[k, rows].astype(jnp.float32) * moved.reshape(Y, Z, X)
                total = term if total is None else total + term

            @pl.when(g == 0)
            def _():
                dst[slot] = total

            @pl.when(g > 0)
            def _():
                dst[slot] = dst[slot] + total
            return carry

        lax.fori_loop(0, K // group, body, 0)

    def fold(full):
        top = jnp.max(full, axis=0)
        rows8 = functools.reduce(jnp.maximum, [top[z : z + 8] for z in range(0, Z, 8)])
        return functools.reduce(
            jnp.maximum, [rows8[:, x : x + LANES] for x in range(0, X, LANES)])

    def spread(small):
        return jnp.concatenate(
            [jnp.concatenate([small] * (X // LANES), axis=1)] * (Z // 8), axis=0)

    def encode(j):
        top = fold(jnp.abs(acc[1]))
        scale_out[j] = top * (1.0 / TOP)
        up = spread(jnp.where(top > 0.0, TOP / top, 0.0))
        for y in range(Y):
            whole = jnp.round(jnp.clip(acc[1, y] * up, -TOP, TOP)).astype(jnp.int32)
            part_out[j, y] = whole.astype(jnp.int16)

    def decoded(j):
        down = spread(scale_in[j])
        return part_in[j].astype(jnp.int32).astype(jnp.float32) * down[None]

    def part_copies(j, slot):
        return [
            pltpu.make_async_remote_copy(
                src_ref=src.at[j], dst_ref=dst.at[slot], send_sem=send.at[j],
                recv_sem=recv.at[slot], device_id={"off": j}, device_id_type=MESH)
            for src, dst, send, recv in (
                (scale_out, scale_in, s_send, s_recv), (part_out, part_in, p_send, p_recv))
        ]

    img_load(me).wait()
    partial(me, acc, 0)

    for t in range(1, n):
        for j, ok, onward, slot, side in (
            (me - t, me - t >= 0, me < n - 1, 1, "r"),
            (me + t, me + t < n, me > 0, 0, "l"),
        ):
            @pl.when(ok)
            def _():
                bg_copy(j, side, slot).wait_recv()

                @pl.when(onward)
                def _():
                    bg_copy(j, side, slot).start()
        for j, ok in ((me - t, me - t >= 0), (me + t, me + t < n)):
            @pl.when(ok)
            def _():
                img_load(j).wait()
                partial(j, acc, 1)
                encode(j)
                for copy in part_copies(j, me):
                    copy.start()

    ld_prev.wait()
    ld_cour.wait()
    for side in "lrud":
        @pl.when(has[side])
        def _():
            halo_copy(side).wait_send()
            pltpu.make_async_remote_copy(
                src_ref=wext.at[mine[side][0], mine[side][1], :],
                dst_ref=wext.at[edge[side][0], edge[side][1], :],
                send_sem=halo_send.at[num[side]], recv_sem=halo_recv.at[num[side]],
                device_id=near[side], device_id_type=MESH).wait_recv()

    lane = lax.broadcasted_iota(jnp.int32, (Z, X), 1)

    def plane(y, carry):
        centre = wext[y + R, pl.ds(8, Z), :]
        running = 3.0 * STENCIL[0] * centre
        for r in range(1, R + 1):
            beside = wext[y + R + r, pl.ds(8, Z), :] + wext[y + R - r, pl.ds(8, Z), :]
            beside = beside + wext[y + R, pl.ds(8 + r, Z), :]
            beside = beside + wext[y + R, pl.ds(8 - r, Z), :]
            beside = beside + jnp.where(lane < X - r, pltpu.roll(centre, X - r, 1), 0.0)
            beside = beside + jnp.where(lane >= r, pltpu.roll(centre, r, 1), 0.0)
            running = running + STENCIL[r] * beside
        fin[y] = 2.0 * centre - prev[y] + cour[y] * (running + acc[0, y])
        return carry

    lax.fori_loop(0, Y, plane, 0)

    for t in range(1, n):
        for j, ok in ((me - t, me - t >= 0), (me + t, me + t < n)):
            @pl.when(ok)
            def _():
                for copy in part_copies(j, j):
                    copy.wait_recv()
                fin[...] = fin[...] + cour[...] * decoded(j)
    out_ref[0] = fin[...]

    for slot, side in enumerate("lr"):
        @pl.when(has[side])
        def _():
            bg_copy(me, side, slot).wait_send()
    for t in range(1, n):
        for j, ok, onward, slot, side in (
            (me - t, me - t >= 0, me < n - 1, 1, "r"),
            (me + t, me + t < n, me > 0, 0, "l"),
        ):
            @pl.when(ok)
            def _():
                for copy in part_copies(j, me):
                    copy.wait_send()

                @pl.when(onward)
                def _():
                    bg_copy(j, side, slot).wait_send()


def on_device(n, nd, image, offset_of, background, wave_now, wave_prev, courant):
    K, rows, Z, X = image.shape
    Y = wave_now.shape[1]
    f32 = jnp.float32
    anywhere = pl.BlockSpec(memory_space=pltpu.HBM)
    dma = pltpu.SemaphoreType.DMA
    return pl.pallas_call(
        functools.partial(kernel, n, nd),
        out_shape=jax.ShapeDtypeStruct(wave_now.shape, f32),
        in_specs=[pl.BlockSpec(memory_space=pltpu.SMEM)] + [anywhere] * 5,
        out_specs=pl.BlockSpec(memory_space=pltpu.VMEM),
        scratch_shapes=[
            pltpu.VMEM((K, rows, Z, X), jnp.bfloat16),
            pltpu.VMEM((n, Y, Z, X), jnp.bfloat16),
            pltpu.VMEM((Y + 2 * R, Z + 16, X), f32),
            pltpu.VMEM((Y, Z, X), f32),
            pltpu.VMEM((Y, Z, X), f32),
            pltpu.VMEM((K, X, X), jnp.bfloat16),
            pltpu.VMEM((2, Y, Z, X), f32),
            pltpu.VMEM((Y, Z, X), f32),
            pltpu.VMEM((n, Y, Z, X), jnp.int16),
            pltpu.VMEM((n, Y, Z, X), jnp.int16),
            pltpu.VMEM((n, 8, LANES), f32),
            pltpu.VMEM((n, 8, LANES), f32),
            dma((4,)), dma((n,)), dma((2, n)), dma((n,)), dma((4,)), dma((4,)),
            dma((n,)), dma((n,)), dma((n,)), dma((n,)),
        ],
        compiler_params=pltpu.CompilerParams(
            collective_id=0, has_side_effects=True, vmem_limit_bytes=67043328),
        name="born_step",
    )(offset_of, image, background, wave_now, wave_prev, courant)


def solution(mesh):
    wave = P(("parts", "shot"), "off", "depth", None)
    return jax.shard_map(
        functools.partial(on_device, mesh.shape["off"], mesh.shape["depth"]),
        mesh=mesh,
        in_specs=(
            P("off", None, "depth", None),
            P("off"),
            wave,
            wave,
            wave,
            P("off", "depth", None),
        ),
        out_specs=wave,
        check_vma=False,
    )
```

```python
import functools

import jax
import jax.numpy as jnp
from jax import lax
from jax.experimental import pallas as pl
from jax.experimental.pallas import tpu as pltpu
from jax.sharding import PartitionSpec as P

H = 64
STENCIL = (-205.0 / 72.0, 8.0 / 5.0, -1.0 / 5.0, 8.0 / 315.0, -1.0 / 560.0)
R = 4
LANES = 128
TOP = 32767.0
PIECES = 2
MESH = pl.DeviceIdType.MESH


def kernel(
    n, nd,
    off_ref, img_hbm, bg_hbm, now_hbm, prev_hbm, cour_hbm,
    out_ref,
    img, bg, wext, prev, cour, shift, acc, part_out, part_in, scale_out, scale_in,
    load_sem, img_sem, bg_send, bg_recv, halo_send, halo_recv, p_send, p_recv, s_send, s_recv,
):
    K, _, Z, X = img.shape
    Y = out_ref.shape[1]
    me = lax.axis_index("off")
    dep = lax.axis_index("depth")
    has = {"l": me > 0, "r": me < n - 1, "u": dep > 0, "d": dep < nd - 1}
    near = {"l": {"off": me - 1}, "r": {"off": me + 1},
            "u": {"depth": dep - 1}, "d": {"depth": dep + 1}}

    fin = out_ref.at[0]

    own = wext.at[pl.ds(R, Y), pl.ds(8, Z), :]
    ld_bg = pltpu.make_async_copy(bg_hbm.at[0], bg.at[me], load_sem.at[0])
    ld_now = pltpu.make_async_copy(now_hbm.at[0], own, load_sem.at[1])
    ld_prev = pltpu.make_async_copy(prev_hbm.at[0], prev, load_sem.at[2])
    ld_cour = pltpu.make_async_copy(cour_hbm, cour, load_sem.at[3])
    ld_bg.start()
    ld_now.start()

    def img_load(j):
        rows = pl.ds(j * Y, Y)
        return pltpu.make_async_copy(img_hbm.at[:, rows], img.at[:, rows], img_sem.at[j])

    img_load(me).start()
    for t in range(1, n):
        @pl.when(me - t >= 0)
        def _():
            img_load(me - t).start()

        @pl.when(me + t < n)
        def _():
            img_load(me + t).start()
    ld_prev.start()
    ld_cour.start()

    barrier = pltpu.get_barrier_semaphore()
    for side in "lrud":
        @pl.when(has[side])
        def _():
            pl.semaphore_signal(barrier, inc=1, device_id=near[side], device_id_type=MESH)

    def clear(rows, cols):
        wext[rows, cols, :] = jnp.zeros((rows.size, cols.size, X), jnp.float32)

    edge = {"l": (pl.ds(0, R), pl.ds(8, Z)), "r": (pl.ds(R + Y, R), pl.ds(8, Z)),
            "u": (pl.ds(R, Y), pl.ds(0, 8)), "d": (pl.ds(R, Y), pl.ds(8 + Z, 8))}
    for side in "lrud":
        @pl.when(jnp.logical_not(has[side]))
        def _():
            clear(*edge[side])

    lead = lax.broadcasted_iota(jnp.int32, (X, X), 1) - lax.broadcasted_iota(jnp.int32, (X, X), 0)

    def build(k, carry):
        h = off_ref[k] - H // 2
        shift[k] = jnp.where(lead == h, 1.0, 0.0).astype(jnp.bfloat16)
        return carry

    lax.fori_loop(0, K, build, 0)
    ld_bg.wait()
    ld_now.wait()
    count = sum(has[s].astype(jnp.int32) for s in "lrud")
    pl.semaphore_wait(barrier, count)

    step = Y // PIECES if Y % PIECES == 0 else Y
    pieces = Y // step

    def bg_copy(j, c, target, slot):
        block = bg.at[j, pl.ds(c * step, step)]
        return pltpu.make_async_remote_copy(
            src_ref=block, dst_ref=block, send_sem=bg_send.at[slot, j * pieces + c],
            recv_sem=bg_recv.at[j * pieces + c], device_id={"off": target},
            device_id_type=MESH)

    mine = {"l": (pl.ds(R, R), pl.ds(8, Z)), "r": (pl.ds(Y, R), pl.ds(8, Z)),
            "u": (pl.ds(R, Y), pl.ds(8, 8)), "d": (pl.ds(R, Y), pl.ds(Z, 8))}
    other = {"l": "r", "r": "l", "u": "d", "d": "u"}
    num = {"l": 0, "r": 1, "u": 2, "d": 3}

    def halo_copy(side):
        there = other[side]
        return pltpu.make_async_remote_copy(
            src_ref=wext.at[mine[side][0], mine[side][1], :],
            dst_ref=wext.at[edge[there][0], edge[there][1], :],
            send_sem=halo_send.at[num[side]], recv_sem=halo_recv.at[num[there]],
            device_id=near[side], device_id_type=MESH)

    for c in range(pieces):
        for slot, side in enumerate("lr"):
            @pl.when(has[side])
            def _():
                bg_copy(me, c, near[side]["off"], slot).start()
    for side in "ud":
        @pl.when(has[side])
        def _():
            halo_copy(side).start()


    group = 4 if K % 4 == 0 else 1

    def partial(j, dst, slot):
        lhs = bg[j].reshape(Y * Z, X)
        rows = pl.ds(j * Y, Y)

        def body(g, carry):
            total = None
            for m in range(group):
                k = g * group + m
                moved = jnp.dot(lhs, shift[k], preferred_element_type=jnp.float32)
                term = img[k, rows].astype(jnp.float32) * moved.reshape(Y, Z, X)
                total = term if total is None else total + term

            @pl.when(g == 0)
            def _():
                dst[slot] = total

            @pl.when(g > 0)
            def _():
                dst[slot] = dst[slot] + total
            return carry

        lax.fori_loop(0, K // group, body, 0)

    def fold(full):
        top = jnp.max(full, axis=0)
        rows8 = functools.reduce(jnp.maximum, [top[z : z + 8] for z in range(0, Z, 8)])
        return functools.reduce(
            jnp.maximum, [rows8[:, x : x + LANES] for x in range(0, X, LANES)])

    def spread(small):
        return jnp.concatenate(
            [jnp.concatenate([small] * (X // LANES), axis=1)] * (Z // 8), axis=0)

    def encode(j):
        top = fold(jnp.abs(acc[1]))
        scale_out[j] = top * (1.0 / TOP)
        up = spread(jnp.where(top > 0.0, TOP / top, 0.0))
        for y in range(Y):
            whole = jnp.round(jnp.clip(acc[1, y] * up, -TOP, TOP)).astype(jnp.int32)
            part_out[j, y] = whole.astype(jnp.int16)

    def decoded(j):
        down = spread(scale_in[j])
        return part_in[j].astype(jnp.int32).astype(jnp.float32) * down[None]

    def part_copies(j, slot):
        return [
            pltpu.make_async_remote_copy(
                src_ref=src.at[j], dst_ref=dst.at[slot], send_sem=send.at[j],
                recv_sem=recv.at[slot], device_id={"off": j}, device_id_type=MESH)
            for src, dst, send, recv in (
                (scale_out, scale_in, s_send, s_recv), (part_out, part_in, p_send, p_recv))
        ]

    def arrivals(t):
        return ((me - t, me - t >= 0, 1), (me + t, me + t < n, -1))

    def onward(t, sign):
        if t % 2 == 0:
            return ()
        spots = [(me + hop * sign, slot) for slot, hop in ((1, 2), (0, 1))]
        return [(to, jnp.logical_and(to >= 0, to < n), slot) for to, slot in spots]

    img_load(me).wait()
    partial(me, acc, 0)

    def send_partial(j, ok):
        @pl.when(ok)
        def _():
            img_load(j).wait()
            partial(j, acc, 1)
            encode(j)
            for copy in part_copies(j, me):
                copy.start()

    for t in range(1, n):
        for c in range(pieces):
            for j, ok, sign in arrivals(t):
                @pl.when(ok)
                def _():
                    bg_copy(j, c, me, 0).wait_recv()
            for j, ok, sign in arrivals(t):
                for to, there, slot in onward(t, sign):
                    @pl.when(jnp.logical_and(ok, there))
                    def _():
                        bg_copy(j, c, to, slot).start()
        if t == 1:
            for side in "lr":
                @pl.when(has[side])
                def _():
                    halo_copy(side).start()
        for j, ok, sign in arrivals(t):
            send_partial(j, ok)

    ld_prev.wait()
    ld_cour.wait()
    for side in "lrud":
        @pl.when(has[side])
        def _():
            halo_copy(side).wait_send()
            pltpu.make_async_remote_copy(
                src_ref=wext.at[mine[side][0], mine[side][1], :],
                dst_ref=wext.at[edge[side][0], edge[side][1], :],
                send_sem=halo_send.at[num[side]], recv_sem=halo_recv.at[num[side]],
                device_id=near[side], device_id_type=MESH).wait_recv()

    lane = lax.broadcasted_iota(jnp.int32, (Z, X), 1)

    def plane(y, carry):
        centre = wext[y + R, pl.ds(8, Z), :]
        running = 3.0 * STENCIL[0] * centre
        for r in range(1, R + 1):
            beside = wext[y + R + r, pl.ds(8, Z), :] + wext[y + R - r, pl.ds(8, Z), :]
            beside = beside + wext[y + R, pl.ds(8 + r, Z), :]
            beside = beside + wext[y + R, pl.ds(8 - r, Z), :]
            beside = beside + jnp.where(lane < X - r, pltpu.roll(centre, X - r, 1), 0.0)
            beside = beside + jnp.where(lane >= r, pltpu.roll(centre, r, 1), 0.0)
            running = running + STENCIL[r] * beside
        fin[y] = 2.0 * centre - prev[y] + cour[y] * (running + acc[0, y])
        return carry

    lax.fori_loop(0, Y, plane, 0)

    for t in range(1, n):
        for j, ok in ((me - t, me - t >= 0), (me + t, me + t < n)):
            @pl.when(ok)
            def _():
                for copy in part_copies(j, j):
                    copy.wait_recv()
                fin[...] = fin[...] + cour[...] * decoded(j)

    for c in range(pieces):
        for slot, side in enumerate("lr"):
            @pl.when(has[side])
            def _():
                bg_copy(me, c, near[side]["off"], slot).wait_send()
    for t in range(1, n):
        for j, ok, sign in arrivals(t):
            @pl.when(ok)
            def _():
                for copy in part_copies(j, me):
                    copy.wait_send()
            for to, there, slot in onward(t, sign):
                @pl.when(jnp.logical_and(ok, there))
                def _():
                    for c in range(pieces):
                        bg_copy(j, c, to, slot).wait_send()


def on_device(n, nd, image, offset_of, background, wave_now, wave_prev, courant):
    K, rows, Z, X = image.shape
    Y = wave_now.shape[1]
    f32 = jnp.float32
    anywhere = pl.BlockSpec(memory_space=pltpu.HBM)
    dma = pltpu.SemaphoreType.DMA
    return pl.pallas_call(
        functools.partial(kernel, n, nd),
        out_shape=jax.ShapeDtypeStruct(wave_now.shape, f32),
        in_specs=[pl.BlockSpec(memory_space=pltpu.SMEM)] + [anywhere] * 5,
        out_specs=pl.BlockSpec(memory_space=pltpu.VMEM),
        scratch_shapes=[
            pltpu.VMEM((K, rows, Z, X), jnp.bfloat16),
            pltpu.VMEM((n, Y, Z, X), jnp.bfloat16),
            pltpu.VMEM((Y + 2 * R, Z + 16, X), f32),
            pltpu.VMEM((Y, Z, X), f32),
            pltpu.VMEM((Y, Z, X), f32),
            pltpu.VMEM((K, X, X), jnp.bfloat16),
            pltpu.VMEM((2, Y, Z, X), f32),
            pltpu.VMEM((n, Y, Z, X), jnp.int16),
            pltpu.VMEM((n, Y, Z, X), jnp.int16),
            pltpu.VMEM((n, 8, LANES), f32),
            pltpu.VMEM((n, 8, LANES), f32),
            dma((4,)), dma((n,)), dma((2, n * PIECES)), dma((n * PIECES,)), dma((4,)), dma((4,)),
            dma((n,)), dma((n,)), dma((n,)), dma((n,)),
        ],
        compiler_params=pltpu.CompilerParams(
            collective_id=0, has_side_effects=True, vmem_limit_bytes=50331648),
        name="born_step",
    )(*[pltpu.with_memory_space_constraint(a, pltpu.HBM) for a in
        (offset_of, image, background, wave_now, wave_prev, courant)])


def solution(mesh):
    wave = P(("parts", "shot"), "off", "depth", None)
    return jax.shard_map(
        functools.partial(on_device, mesh.shape["off"], mesh.shape["depth"]),
        mesh=mesh,
        in_specs=(
            P("off", None, "depth", None),
            P("off"),
            wave,
            wave,
            wave,
            P("off", "depth", None),
        ),
        out_specs=wave,
        check_vma=False,
    )
```

```python
import functools

import jax
import jax.numpy as jnp
from jax import lax
from jax.experimental import pallas as pl
from jax.experimental.pallas import tpu as pltpu
from jax.sharding import PartitionSpec as P

H = 64
STENCIL = (-205.0 / 72.0, 8.0 / 5.0, -1.0 / 5.0, 8.0 / 315.0, -1.0 / 560.0)
R = 4
LANES = 128
TOP = 32767.0
PIECES = 4
MESH = pl.DeviceIdType.MESH


def kernel(
    n, nd,
    off_ref, img_hbm, bg_hbm, now_hbm, prev_hbm, cour_hbm,
    out_ref,
    img, bg, wext, prev, cour, shift, acc, part_out, part_in, scale_out, scale_in,
    load_sem, img_sem, bg_send, bg_recv, halo_send, halo_recv, p_send, p_recv, s_send, s_recv,
):
    K, _, Z, X = img.shape
    Y = out_ref.shape[1]
    me = lax.axis_index("off")
    dep = lax.axis_index("depth")
    has = {"l": me > 0, "r": me < n - 1, "u": dep > 0, "d": dep < nd - 1}
    near = {"l": {"off": me - 1}, "r": {"off": me + 1},
            "u": {"depth": dep - 1}, "d": {"depth": dep + 1}}

    fin = out_ref.at[0]

    own = wext.at[pl.ds(R, Y), pl.ds(8, Z), :]
    ld_bg = pltpu.make_async_copy(bg_hbm.at[0], bg.at[me], load_sem.at[0])
    ld_now = pltpu.make_async_copy(now_hbm.at[0], own, load_sem.at[1])
    ld_prev = pltpu.make_async_copy(prev_hbm.at[0], prev, load_sem.at[2])
    ld_cour = pltpu.make_async_copy(cour_hbm, cour, load_sem.at[3])
    ld_bg.start()
    ld_now.start()

    def img_load(j):
        rows = pl.ds(j * Y, Y)
        return pltpu.make_async_copy(img_hbm.at[:, rows], img.at[:, rows], img_sem.at[j])

    img_load(me).start()
    for t in range(1, n):
        @pl.when(me - t >= 0)
        def _():
            img_load(me - t).start()

        @pl.when(me + t < n)
        def _():
            img_load(me + t).start()
    ld_prev.start()
    ld_cour.start()

    barrier = pltpu.get_barrier_semaphore()
    for side in "lrud":
        @pl.when(has[side])
        def _():
            pl.semaphore_signal(barrier, inc=1, device_id=near[side], device_id_type=MESH)

    def clear(rows, cols):
        wext[rows, cols, :] = jnp.zeros((rows.size, cols.size, X), jnp.float32)

    edge = {"l": (pl.ds(0, R), pl.ds(8, Z)), "r": (pl.ds(R + Y, R), pl.ds(8, Z)),
            "u": (pl.ds(R, Y), pl.ds(0, 8)), "d": (pl.ds(R, Y), pl.ds(8 + Z, 8))}
    for side in "lrud":
        @pl.when(jnp.logical_not(has[side]))
        def _():
            clear(*edge[side])

    lead = lax.broadcasted_iota(jnp.int32, (X, X), 1) - lax.broadcasted_iota(jnp.int32, (X, X), 0)

    def build(k, carry):
        h = off_ref[k] - H // 2
        shift[k] = jnp.where(lead == h, 1.0, 0.0).astype(jnp.bfloat16)
        return carry

    lax.fori_loop(0, K, build, 0)
    ld_bg.wait()
    ld_now.wait()
    count = sum(has[s].astype(jnp.int32) for s in "lrud")
    pl.semaphore_wait(barrier, count)

    step = Y // PIECES if Y % PIECES == 0 else Y
    pieces = Y // step

    def bg_copy(j, c, target, slot):
        block = bg.at[j, pl.ds(c * step, step)]
        return pltpu.make_async_remote_copy(
            src_ref=block, dst_ref=block, send_sem=bg_send.at[slot, j * pieces + c],
            recv_sem=bg_recv.at[j * pieces + c], device_id={"off": target},
            device_id_type=MESH)

    mine = {"l": (pl.ds(R, R), pl.ds(8, Z)), "r": (pl.ds(Y, R), pl.ds(8, Z)),
            "u": (pl.ds(R, Y), pl.ds(8, 8)), "d": (pl.ds(R, Y), pl.ds(Z, 8))}
    other = {"l": "r", "r": "l", "u": "d", "d": "u"}
    num = {"l": 0, "r": 1, "u": 2, "d": 3}

    def halo_copy(side):
        there = other[side]
        return pltpu.make_async_remote_copy(
            src_ref=wext.at[mine[side][0], mine[side][1], :],
            dst_ref=wext.at[edge[there][0], edge[there][1], :],
            send_sem=halo_send.at[num[side]], recv_sem=halo_recv.at[num[there]],
            device_id=near[side], device_id_type=MESH)

    for c in range(pieces):
        for slot, side in enumerate("lr"):
            @pl.when(has[side])
            def _():
                bg_copy(me, c, near[side]["off"], slot).start()
    for side in "lrud":
        @pl.when(has[side])
        def _():
            halo_copy(side).start()


    group = 4 if K % 4 == 0 else 1

    def partial(j, dst, slot):
        lhs = bg[j].reshape(Y * Z, X)
        rows = pl.ds(j * Y, Y)

        def body(g, carry):
            total = None
            for m in range(group):
                k = g * group + m
                moved = jnp.dot(lhs, shift[k], preferred_element_type=jnp.float32)
                term = img[k, rows].astype(jnp.float32) * moved.reshape(Y, Z, X)
                total = term if total is None else total + term

            @pl.when(g == 0)
            def _():
                dst[slot] = total

            @pl.when(g > 0)
            def _():
                dst[slot] = dst[slot] + total
            return carry

        lax.fori_loop(0, K // group, body, 0)

    def fold(full):
        top = jnp.max(full, axis=0)
        rows8 = functools.reduce(jnp.maximum, [top[z : z + 8] for z in range(0, Z, 8)])
        return functools.reduce(
            jnp.maximum, [rows8[:, x : x + LANES] for x in range(0, X, LANES)])

    def spread(small):
        return jnp.concatenate(
            [jnp.concatenate([small] * (X // LANES), axis=1)] * (Z // 8), axis=0)

    def encode(j):
        top = fold(jnp.abs(acc[1]))
        scale_out[j] = top * (1.0 / TOP)
        up = spread(jnp.where(top > 0.0, TOP / top, 0.0))
        for y in range(Y):
            whole = jnp.round(jnp.clip(acc[1, y] * up, -TOP, TOP)).astype(jnp.int32)
            part_out[j, y] = whole.astype(jnp.int16)

    def decoded(j):
        down = spread(scale_in[j])
        return part_in[j].astype(jnp.int32).astype(jnp.float32) * down[None]

    def part_copies(j, slot):
        return [
            pltpu.make_async_remote_copy(
                src_ref=src.at[j], dst_ref=dst.at[slot], send_sem=send.at[j],
                recv_sem=recv.at[slot], device_id={"off": j}, device_id_type=MESH)
            for src, dst, send, recv in (
                (scale_out, scale_in, s_send, s_recv), (part_out, part_in, p_send, p_recv))
        ]

    def arrivals(t):
        return ((me - t, me - t >= 0, 1), (me + t, me + t < n, -1))

    def onward(t, sign):
        if t % 2 == 0:
            return ()
        spots = [(me + hop * sign, slot) for slot, hop in ((1, 2), (0, 1))]
        return [(to, jnp.logical_and(to >= 0, to < n), slot) for to, slot in spots]

    img_load(me).wait()
    partial(me, acc, 0)

    def send_partial(j, ok):
        @pl.when(ok)
        def _():
            img_load(j).wait()
            partial(j, acc, 1)
            encode(j)
            for copy in part_copies(j, me):
                copy.start()

    order = [1] + [t for low in range(2, n, 2) for t in (low + 1, low) if t < n]
    for t in order:
        for c in range(pieces):
            for j, ok, sign in arrivals(t):
                @pl.when(ok)
                def _():
                    bg_copy(j, c, me, 0).wait_recv()
            for j, ok, sign in arrivals(t):
                for to, there, slot in onward(t, sign):
                    @pl.when(jnp.logical_and(ok, there))
                    def _():
                        bg_copy(j, c, to, slot).start()
        for j, ok, sign in arrivals(t):
            send_partial(j, ok)

    ld_prev.wait()
    ld_cour.wait()
    for side in "lrud":
        @pl.when(has[side])
        def _():
            halo_copy(side).wait_send()
            pltpu.make_async_remote_copy(
                src_ref=wext.at[mine[side][0], mine[side][1], :],
                dst_ref=wext.at[edge[side][0], edge[side][1], :],
                send_sem=halo_send.at[num[side]], recv_sem=halo_recv.at[num[side]],
                device_id=near[side], device_id_type=MESH).wait_recv()

    lane = lax.broadcasted_iota(jnp.int32, (Z, X), 1)

    def plane(y, carry):
        centre = wext[y + R, pl.ds(8, Z), :]
        running = 3.0 * STENCIL[0] * centre
        for r in range(1, R + 1):
            beside = wext[y + R + r, pl.ds(8, Z), :] + wext[y + R - r, pl.ds(8, Z), :]
            beside = beside + wext[y + R, pl.ds(8 + r, Z), :]
            beside = beside + wext[y + R, pl.ds(8 - r, Z), :]
            beside = beside + jnp.where(lane < X - r, pltpu.roll(centre, X - r, 1), 0.0)
            beside = beside + jnp.where(lane >= r, pltpu.roll(centre, r, 1), 0.0)
            running = running + STENCIL[r] * beside
        fin[y] = 2.0 * centre - prev[y] + cour[y] * (running + acc[0, y])
        return carry

    lax.fori_loop(0, Y, plane, 0)

    for t in range(1, n):
        for j, ok in ((me - t, me - t >= 0), (me + t, me + t < n)):
            @pl.when(ok)
            def _():
                for copy in part_copies(j, j):
                    copy.wait_recv()
                fin[...] = fin[...] + cour[...] * decoded(j)

    for c in range(pieces):
        for slot, side in enumerate("lr"):
            @pl.when(has[side])
            def _():
                bg_copy(me, c, near[side]["off"], slot).wait_send()
    for t in range(1, n):
        for j, ok, sign in arrivals(t):
            @pl.when(ok)
            def _():
                for copy in part_copies(j, me):
                    copy.wait_send()
            for to, there, slot in onward(t, sign):
                @pl.when(jnp.logical_and(ok, there))
                def _():
                    for c in range(pieces):
                        bg_copy(j, c, to, slot).wait_send()


def on_device(n, nd, image, offset_of, background, wave_now, wave_prev, courant):
    K, rows, Z, X = image.shape
    Y = wave_now.shape[1]
    f32 = jnp.float32
    anywhere = pl.BlockSpec(memory_space=pltpu.HBM)
    dma = pltpu.SemaphoreType.DMA
    return pl.pallas_call(
        functools.partial(kernel, n, nd),
        out_shape=jax.ShapeDtypeStruct(wave_now.shape, f32),
        in_specs=[pl.BlockSpec(memory_space=pltpu.SMEM)] + [anywhere] * 5,
        out_specs=pl.BlockSpec(memory_space=pltpu.VMEM),
        scratch_shapes=[
            pltpu.VMEM((K, rows, Z, X), jnp.bfloat16),
            pltpu.VMEM((n, Y, Z, X), jnp.bfloat16),
            pltpu.VMEM((Y + 2 * R, Z + 16, X), f32),
            pltpu.VMEM((Y, Z, X), f32),
            pltpu.VMEM((Y, Z, X), f32),
            pltpu.VMEM((K, X, X), jnp.bfloat16),
            pltpu.VMEM((2, Y, Z, X), f32),
            pltpu.VMEM((n, Y, Z, X), jnp.int16),
            pltpu.VMEM((n, Y, Z, X), jnp.int16),
            pltpu.VMEM((n, 8, LANES), f32),
            pltpu.VMEM((n, 8, LANES), f32),
            dma((4,)), dma((n,)), dma((2, n * PIECES)), dma((n * PIECES,)), dma((4,)), dma((4,)),
            dma((n,)), dma((n,)), dma((n,)), dma((n,)),
        ],
        compiler_params=pltpu.CompilerParams(
            collective_id=0, has_side_effects=True, vmem_limit_bytes=50331648),
        name="born_step",
    )(*[pltpu.with_memory_space_constraint(a, pltpu.HBM) for a in
        (offset_of, image, background, wave_now, wave_prev, courant)])


def solution(mesh):
    wave = P(("parts", "shot"), "off", "depth", None)
    return jax.shard_map(
        functools.partial(on_device, mesh.shape["off"], mesh.shape["depth"]),
        mesh=mesh,
        in_specs=(
            P("off", None, "depth", None),
            P("off"),
            wave,
            wave,
            wave,
            P("off", "depth", None),
        ),
        out_specs=wave,
        check_vma=False,
    )
```
